32 devices in a mesh: lat: 4 (over z), lon: 8 (over y, x, core).
Axes of the slice: x: 2, y: 2, z: 4, core: 2. Of those that a mesh axis runs over, the one named last changes fastest.
Arguments:
- inputs: bfloat16 [128, 360, 512], P('lat', 'lon'), may hold values from -6 to 6
- metric: float32 [128, 360], P('lat', 'lon'), may hold values from 0.5 to 2
- kernel_one: float32 [9, 512], replicated, may hold values from -2 to 2
- kernel_two: float32 [9, 512], replicated, may hold values from -2 to 2
- widths: int32 [128], P('lat'), may hold values from 0 to 90, as said below
- zonal_gains: bfloat16 [128, 181], P('lat'), may hold values from -0.19921875 to 0.19921875
- norm_gain: float32 [512], replicated, may hold values from 0.5 to 1.5
- weight_in: bfloat16 [512, 1024], replicated, may hold values from -0.25 to 0.25
- weight_out: bfloat16 [1024, 512], replicated, may hold values from -0.1875 to 0.1875
Outputs:
- updated: bfloat16 [128, 360, 512], P('lat', 'lon')
The draws below stay inside these ranges and needn't reach their ends.
Inputs may be any that keep to these rules, and one draw needn't show every extreme that they name: widths gives the zonal filter half-width of each latitude row.
All inputs are finite; a program needn't handle non-finite values.
Results may differ from the reference program's by a relative error of at most 0.0061.
Values may be sent and summed in bfloat16 or wider, within the bound.
A program may use at most 64 MiB of HBM per device.

```python
import math
import jax
import jax.numpy as jnp
from jax import lax

C = 512
HID = 1024
NLAT = 128
NLON = 360
BMAX = 90


def draw_widths(key, part):
    row_ids = jnp.arange(NLAT, dtype=jnp.int32)
    distance = jnp.minimum(row_ids, NLAT - 1 - row_ids)
    quarter = NLAT // 4
    base_width = BMAX - distance * BMAX // quarter
    jitter = jax.random.randint(key, (NLAT,), -(BMAX // 8), BMAX // 8 + 1, dtype=jnp.int32)
    result = jnp.clip(base_width + jitter, 0, BMAX)
    result = jnp.where(distance >= quarter, 0, result)
    result = jnp.where(distance == 0, BMAX, result)
    return result.astype(jnp.int32)


def block_scale(rng, shape, cuts, smallest, top_value):
    level = 1.0
    for axis_at, parts in cuts:
        steps = jax.random.uniform(jax.random.fold_in(jax.random.fold_in(rng, 6), axis_at), (parts,), jnp.float32, smallest / len(cuts), top_value / len(cuts))
        level = level * jnp.repeat(jnp.exp(steps), shape[axis_at] // parts).reshape((-1,) + (1,) * (len(shape) - 1 - axis_at))
    return level


def bell_draw(own_key, dims, spread, reach, shards=(), kind=jnp.bfloat16):
    drawn = spread * jax.random.normal(own_key, dims, jnp.float32)
    if shards:
        drawn = drawn * block_scale(own_key, dims, shards, -0.22, 0.18)
    return jnp.clip(drawn, -reach, reach).astype(kind)


def setup_inputs(seed: int = 0) -> dict:
    streams_of = jax.random.split(jax.random.key(seed), 10)
    return {
        "inputs": bell_draw(streams_of[0], (NLAT, NLON, C), 1.0, 6.0, ((0, 4), (1, 8))),
        "metric": jnp.clip(jnp.exp(math.log(2.0) - 1.3862944 * jax.random.uniform(streams_of[1], (NLAT, NLON), jnp.float32) ** block_scale(streams_of[1], (NLAT, NLON), ((0, 4), (1, 8)), -0.2, 0.2)), 0.5, 2.0),
        "kernel_one": bell_draw(streams_of[2], (9, C), 0.35, 2.0, (), jnp.float32),
        "kernel_two": bell_draw(streams_of[3], (9, C), 0.35, 2.0, (), jnp.float32),
        "widths": draw_widths(jax.random.fold_in(streams_of[9], 71), 0),
        "zonal_gains": bell_draw(streams_of[5], (NLAT, 2 * BMAX + 1), 0.04, 0.19921875, ((0, 4),)),
        "norm_gain": jnp.clip(1.0 + 0.1 * jax.random.normal(streams_of[6], (C,), jnp.float32), 0.5, 1.5),
        "weight_in": bell_draw(streams_of[7], (C, HID), C ** -0.5, 0.25),
        "weight_out": bell_draw(streams_of[8], (HID, C), HID ** -0.5, 0.1875),
    }


def gelu_tanh(values):
    return jax.nn.gelu(values, approximate=True)

def extend_whole(field):
    half = field.shape[1] // 2
    top_row = jnp.roll(field[:1], half, axis=1)
    bottom_row = jnp.roll(field[-1:], half, axis=1)
    tall = jnp.concatenate([top_row, field, bottom_row], axis=0)
    return jnp.concatenate([tall[:, -1:], tall, tall[:, :1]], axis=1)

def stencil(extended, kernel):
    height = extended.shape[0] - 2
    breadth = extended.shape[1] - 2
    summed = jnp.zeros((height, breadth, extended.shape[2]), jnp.float32)
    for tap in range(9):
        row_shift = tap // 3
        col_shift = tap % 3
        piece = extended[row_shift:row_shift + height, col_shift:col_shift + breadth].astype(jnp.float32)
        summed = summed + kernel[tap] * piece
    return summed

def tap_matrix(gain_pad, row_width, tap_block, block_len, half_reach):
    first_tap = (tap_block * block_len).astype(jnp.int32)
    segment = lax.dynamic_slice_in_dim(gain_pad, first_tap, block_len, 0)
    tap_ids = first_tap + jnp.arange(block_len, dtype=jnp.int32)
    keep = jnp.abs(tap_ids - half_reach) <= row_width
    segment = jnp.where(keep, segment, jnp.zeros_like(segment))
    padded = jnp.concatenate([segment, jnp.zeros((block_len + 1,), segment.dtype)])
    return jnp.tile(padded, block_len)[:2 * block_len * block_len].reshape(block_len, 2 * block_len)

def zonal_circle(circle, row_width, row_gains, first_block, block_count, active):
    circle_len = circle.shape[0]
    chans = circle.shape[1]
    block_len = circle_len // 8
    half_reach = circle_len // 4
    tap_blocks = 2 * half_reach // block_len + 1
    extended = jnp.concatenate([circle[circle_len - half_reach:], circle, circle[:half_reach + block_len]], axis=0)
    blocked = extended.reshape(-1, block_len, chans)
    gain_pad = jnp.concatenate([row_gains, jnp.zeros((tap_blocks * block_len - row_gains.shape[0],), row_gains.dtype)])
    row_width = row_width.astype(jnp.int32)
    if active:
        start_tap = ((half_reach - row_width) // block_len).astype(jnp.int32)
        stop_tap = ((half_reach + row_width) // block_len + 1).astype(jnp.int32)
    else:
        start_tap = jnp.zeros((), jnp.int32)
        stop_tap = jnp.full((), tap_blocks, jnp.int32)

    def add_block(tap_block, summed):
        matrix = tap_matrix(gain_pad, row_width, tap_block, block_len, half_reach)
        first_window = (first_block + tap_block).astype(jnp.int32)
        near = lax.dynamic_slice_in_dim(blocked, first_window, block_count, 0)
        after = lax.dynamic_slice_in_dim(blocked, first_window + 1, block_count, 0)
        window = jnp.concatenate([near, after], axis=1)
        return summed + jnp.einsum('ab,pbc->pac', matrix.astype(jnp.float32), window.astype(jnp.float32))
    return lax.fori_loop(start_tap, stop_tap, add_block, jnp.zeros((block_count, block_len, chans), jnp.float32))

def reference(inputs, metric, kernel_one, kernel_two, widths, zonal_gains, norm_gain, weight_in, weight_out):
    group = min(64, C)
    groups = C // group
    stacked = inputs.reshape(NLAT, NLON, groups, group).transpose(2, 0, 1, 3)
    kernels_one = kernel_one.reshape(9, groups, group).transpose(1, 0, 2)
    kernels_two = kernel_two.reshape(9, groups, group).transpose(1, 0, 2)

    def stencil_pair(operands):
        field, first_kernel, second_kernel = operands
        first = (field.astype(jnp.float32) * metric[:, :, None]).astype(jnp.bfloat16)
        stencil_one = stencil(extend_whole(first), first_kernel)
        second = (metric[:, :, None] * gelu_tanh(stencil_one)).astype(jnp.bfloat16)
        stencil_two = stencil(extend_whole(second), second_kernel)
        return (field.astype(jnp.float32) + stencil_two).astype(jnp.bfloat16)
    mixed = lax.map(stencil_pair, (stacked, kernels_one, kernels_two))
    mixed = mixed.transpose(1, 2, 0, 3).reshape(NLAT, NLON, C)

    def zonal_row(operands):
        circle, row_width, row_gains = operands
        filtered = zonal_circle(circle, row_width, row_gains, 0, 8, True)
        return filtered.reshape(NLON, C).astype(jnp.bfloat16)
    zonal = lax.map(zonal_row, (mixed, widths, zonal_gains))

    def row_group(operands):
        group_rows, group_zonal = operands
        flat = group_rows.reshape(-1, C).astype(jnp.float32)
        scale = lax.rsqrt(lax.optimization_barrier(jnp.mean(flat * flat, axis=1, keepdims=True)) + 1e-06)
        normed = (flat * scale * norm_gain).astype(jnp.bfloat16)
        hidden = gelu_tanh(jnp.dot(normed, weight_in, preferred_element_type=jnp.float32)).astype(jnp.bfloat16)
        pointwise = jnp.dot(hidden, weight_out, preferred_element_type=jnp.float32)
        combined = flat + group_zonal.reshape(-1, C).astype(jnp.float32) + pointwise
        return combined.astype(jnp.bfloat16).reshape(group_rows.shape)
    updated = lax.map(row_group, (mixed.reshape(NLAT // 8, 8, NLON, C), zonal.reshape(NLAT // 8, 8, NLON, C)))
    return updated.reshape(NLAT, NLON, C)
```

```python
import functools

import jax
import jax.numpy as jnp
from jax import lax
from jax.experimental import pallas as pl
from jax.experimental.pallas import tpu as pltpu
from jax.sharding import PartitionSpec as P

MESH = pl.DeviceIdType.MESH
LANES = 128
LEAD = 8


def round_up(value, step):
    return -(-value // step) * step


def gelu_tanh(values):
    return jax.nn.gelu(values, approximate=True)


def body(
    lats, n, rows, cols, chans, pad, reach,
    x_ref, metric_ref, tb_ref, lr_ref, k1_ref, k2_ref, gains_ref, gain_ref, win_ref, wout_ref,
    out_ref,
    ext, sec, held, acc, mix, circ, zsend, zrecv, side, taps,
    hs_sem, hr_sem, fs_sem, fr_sem, rs_sem, rr_sem,
):
    lat = lax.axis_index("lat")
    me = lax.axis_index("lon")
    chunks = rows // n
    half = n // 2
    wide = ext.shape[1]
    full = ext.shape[2]
    slabs = 2 * reach + 1

    at_top = lat == 0
    at_bottom = lat == lats - 1
    up_lat = jnp.where(at_top, 0, lat - 1)
    up_lon = jnp.where(at_top, lax.rem(me + half, n), me)
    down_lat = jnp.where(at_bottom, lats - 1, lat + 1)
    down_lon = jnp.where(at_bottom, lax.rem(me + half, n), me)
    left = lax.rem(me + n - 1, n)
    right = lax.rem(me + 1, n)

    def before(lon):
        return lax.rem(lon + n - 1, n)

    def after(lon):
        return lax.rem(lon + 1, n)

    def clear(e, carry):
        ext[e, 0:LEAD, :] = jnp.zeros((LEAD, full), jnp.float32)
        return carry

    lax.fori_loop(0, rows + 4, clear, 0)

    barrier = pltpu.get_barrier_semaphore()
    greeted = [
        (lat, left), (lat, right),
        (up_lat, up_lon), (up_lat, before(up_lon)), (up_lat, after(up_lon)),
        (down_lat, down_lon), (down_lat, before(down_lon)), (down_lat, after(down_lon)),
    ] + [(lat, lax.rem(me + o, n)) for o in range(1, n)]
    for device in greeted:
        pl.semaphore_signal(barrier, inc=1, device_id=device, device_id_type=MESH)
    pl.semaphore_wait(barrier, len(greeted))

    halo = []

    def send_halo(src, dst, recv_index, device):
        copy = pltpu.make_async_remote_copy(
            src_ref=src, dst_ref=dst, send_sem=hs_sem.at[len(halo)], recv_sem=hr_sem.at[recv_index],
            device_id=device, device_id_type=MESH,
        )
        copy.start()
        halo.append(copy)

    def slot_row(slot):
        return jnp.where(slot < 2, slot, rows + slot)

    send_halo(lr_ref.at[0], side.at[1, pl.ds(2, rows)], 5, (lat, left))
    send_halo(lr_ref.at[1], side.at[0, pl.ds(2, rows)], 4, (lat, right))
    for i in range(2):
        up_slot = jnp.where(at_top, 1 - i, 2 + i)
        down_slot = jnp.where(at_bottom, 3 - i, i)
        for slot, src_row, device_lat, device_lon in (
            (up_slot, i, up_lat, up_lon),
            (down_slot, rows - 2 + i, down_lat, down_lon),
        ):
            tb = i if src_row < 2 else 2 + i
            dst_row = slot_row(slot)
            send_halo(
                tb_ref.at[tb], ext.at[dst_row, pl.ds(LEAD, pad)], slot, (device_lat, device_lon)
            )
            send_halo(
                lr_ref.at[0, src_row], side.at[1, dst_row], 10 + slot,
                (device_lat, before(device_lon)),
            )
            send_halo(
                lr_ref.at[1, src_row], side.at[0, dst_row], 6 + slot,
                (device_lat, after(device_lon)),
            )

    def place(i, carry):
        weight = metric_ref[i]
        ext[i + 2, pad:wide, :] = jnp.zeros((wide - pad, full), jnp.float32)
        held[i, pad - 8:pad, :] = jnp.zeros((8, chans), jnp.float32)
        ext[i + 2, LEAD:LEAD + cols, chans:] = weight
        for c in range(chans // LANES):
            lanes = slice(c * LANES, (c + 1) * LANES)
            cells = x_ref[i, :, lanes].astype(jnp.float32)
            held[i, 0:cols, lanes] = cells
            ext[i + 2, LEAD:LEAD + cols, lanes] = (
                (cells * weight).astype(jnp.bfloat16).astype(jnp.float32)
            )
        return carry

    lax.fori_loop(0, rows, place, 0)

    tap_lanes = taps.shape[2]
    lane_ids = lax.broadcasted_iota(jnp.int32, (pad, tap_lanes), 1)
    for k in range(chunks):
        line = jnp.broadcast_to(gains_ref[pl.ds(k * n + me, 1), :], (pad, tap_lanes))
        shifted = pltpu.roll(line, 0, 1, stride=1, stride_axis=0)
        total = jnp.zeros((pad, tap_lanes), jnp.float32)
        for d in range(slabs):
            moved = pltpu.roll(shifted, (pad - cols) * d, 1) if d else shifted
            inside = (lane_ids >= pad * d) & (lane_ids < pad * d + cols)
            total = jnp.where(inside, moved, total)
        taps[k] = total.astype(jnp.bfloat16)

    def recv_halo(src, dst, recv_index):
        pltpu.make_async_remote_copy(
            src_ref=src, dst_ref=dst, send_sem=hs_sem.at[0], recv_sem=hr_sem.at[recv_index],
            device_id=(lat, right), device_id_type=MESH,
        ).wait_recv()

    for s in range(2):
        recv_halo(lr_ref.at[s], side.at[s, pl.ds(2, rows)], 4 + s)
    for slot in range(4):
        row = slot if slot < 2 else rows + slot
        recv_halo(tb_ref.at[0], ext.at[row, pl.ds(LEAD, pad)], slot)
        for s in range(2):
            recv_halo(lr_ref.at[0, 0], side.at[s, row], 6 + 4 * s + slot)

    def join(e, carry):
        ext[e, LEAD - 2:LEAD, :] = side[0, e]
        ext[e, LEAD + cols:LEAD + cols + 2, :] = side[1, e]
        return carry

    lax.fori_loop(0, rows + 4, join, 0)

    def stencil(src, row, kernel, lanes):
        sums = [None, None, None]
        for a in range(3):
            line = src[row + a, :, lanes]
            for b in range(3):
                term = kernel(3 * a + b, lanes) * line
                sums[b] = term if sums[b] is None else sums[b] + term
        return pltpu.roll(sums[0], 1, 0) + sums[1] + pltpu.roll(sums[2], wide - 1, 0)

    def second_row(p, carry):
        flip = ((p == 0) & at_top) | ((p == rows + 1) & at_bottom)
        which = jnp.where(flip, 1, 0)
        weight = ext[p + 1, :, chans:]
        for c in range(chans // LANES):
            lanes = slice(c * LANES, (c + 1) * LANES)
            value = stencil(ext, p, lambda t, l: k1_ref[which, t:t + 1, l], lanes)
            value = weight * gelu_tanh(value)
            sec[p, :, lanes] = value.astype(jnp.bfloat16).astype(jnp.float32)
        return carry

    col_ids = lax.broadcasted_iota(jnp.int32, (pad, LANES), 0)

    def mixed_row(i, carry):
        for c in range(chans // LANES):
            lanes = slice(c * LANES, (c + 1) * LANES)
            value = stencil(sec, i, lambda t, l: k2_ref[t:t + 1, l], lanes)
            value = held[i, :, lanes] + value[LEAD:, :]
            mix[i, :, lanes] = jnp.where(col_ids < cols, value, 0.0).astype(jnp.bfloat16)
        return carry

    forward = []
    for k in range(chunks):
        start = 0 if k == 0 else k * n + 2
        lax.fori_loop(start, (k + 1) * n + 2, second_row, 0)
        lax.fori_loop(k * n, (k + 1) * n, mixed_row, 0)
        for o in range(1, n):
            target = lax.rem(me + o, n)
            copy = pltpu.make_async_remote_copy(
                src_ref=mix.at[k * n + target], dst_ref=circ.at[k, me + reach],
                send_sem=fs_sem.at[k, o], recv_sem=fr_sem.at[k, o],
                device_id=(lat, target), device_id_type=MESH,
            )
            copy.start()
            forward.append(copy)
        circ[k, me + reach] = mix[k * n + me]

    group = 8

    def network(g, carry):
        flat = mix[pl.ds(g * group, group)].reshape(group * pad, chans).astype(jnp.float32)
        scale = lax.rsqrt(jnp.mean(flat * flat, axis=1, keepdims=True) + 1e-06)
        normed = (flat * scale * gain_ref[...]).astype(jnp.bfloat16)
        hidden = gelu_tanh(
            jnp.dot(normed, win_ref[...], preferred_element_type=jnp.float32)
        ).astype(jnp.bfloat16)
        point = jnp.dot(hidden, wout_ref[...], preferred_element_type=jnp.float32)
        acc[pl.ds(g * group, group)] = (flat + point).reshape(group, pad, chans)
        return carry

    lax.fori_loop(0, rows // group, network, 0)

    back = []
    for k in range(chunks):
        for o in range(1, n):
            source = lax.rem(me + n - o, n)
            pltpu.make_async_remote_copy(
                src_ref=mix.at[k * n], dst_ref=circ.at[k, source + reach],
                send_sem=fs_sem.at[k, o], recv_sem=fr_sem.at[k, o],
                device_id=(lat, source), device_id_type=MESH,
            ).wait_recv()
        for e in range(reach):
            circ[k, e] = circ[k, n + e]
            circ[k, n + reach + e] = circ[k, reach + e]

        def filter_block(a, carry):
            window = circ[k, pl.ds(a, slabs)].reshape(slabs * pad, chans)
            result = jnp.dot(
                taps[k, :, 0:slabs * pad], window, preferred_element_type=jnp.float32
            )
            zsend[k * n + a] = result.astype(jnp.bfloat16)
            return carry

        lax.fori_loop(0, n, filter_block, 0, unroll=4)
        for o in range(1, n):
            target = lax.rem(me + o, n)
            copy = pltpu.make_async_remote_copy(
                src_ref=zsend.at[k * n + target], dst_ref=zrecv.at[k * n + me],
                send_sem=rs_sem.at[k, o], recv_sem=rr_sem.at[k, o],
                device_id=(lat, target), device_id_type=MESH,
            )
            copy.start()
            back.append(copy)
        zrecv[k * n + me] = zsend[k * n + me]

    for k in range(chunks):
        for o in range(1, n):
            source = lax.rem(me + n - o, n)
            pltpu.make_async_remote_copy(
                src_ref=zsend.at[k * n], dst_ref=zrecv.at[k * n + source],
                send_sem=rs_sem.at[k, o], recv_sem=rr_sem.at[k, o],
                device_id=(lat, source), device_id_type=MESH,
            ).wait_recv()

        def finish(i, carry):
            out_ref[i] = (acc[i] + zrecv[i].astype(jnp.float32)).astype(jnp.bfloat16)
            return carry

        lax.fori_loop(k * n, (k + 1) * n, finish, 0)

    for copy in halo + forward + back:
        copy.wait_send()


def local(
    lats, n,
    inputs, metric, kernel_one, kernel_two, widths, zonal_gains, norm_gain, weight_in, weight_out
):
    rows, cols, chans = inputs.shape
    pad = round_up(cols, 16)
    wide = LEAD + pad
    full = chans + LANES
    reach = n // 4
    slabs = 2 * reach + 1
    count = zonal_gains.shape[1]
    center = (count - 1) // 2
    tap_lanes = round_up(max(slabs * pad, count + pad - 1), LANES)

    def packed(cells, weights):
        weights = weights[:, :, None]
        first = (cells.astype(jnp.float32) * weights).astype(jnp.bfloat16).astype(jnp.float32)
        spread = jnp.broadcast_to(weights, weights.shape[:2] + (LANES,))
        return jnp.concatenate([first, spread], axis=2)

    spread = jnp.broadcast_to(metric[:, :, None], (rows, cols, LANES))
    edge_cells = jnp.concatenate([inputs[:2], inputs[-2:]], axis=0)
    edge_weights = jnp.concatenate([metric[:2], metric[-2:]], axis=0)
    tb = jnp.pad(packed(edge_cells, edge_weights), ((0, 0), (0, pad - cols), (0, 0)))
    lr = jnp.stack(
        [packed(inputs[:, :2], metric[:, :2]), packed(inputs[:, -2:], metric[:, -2:])]
    )
    flipped = kernel_one.reshape(3, 3, chans)[::-1].reshape(9, chans)
    k_one = jnp.stack([kernel_one, flipped])
    offsets = jnp.abs(jnp.arange(count, dtype=jnp.int32) - center)
    kept = jnp.where(
        offsets[None, :] <= widths[:, None], zonal_gains.astype(jnp.float32), 0.0
    )
    kept = jnp.pad(kept, ((0, 0), (0, tap_lanes - count)))
    chunks = rows // n
    vmem = pl.BlockSpec(memory_space=pltpu.VMEM)
    sem = pltpu.SemaphoreType.DMA
    out = pl.pallas_call(
        functools.partial(body, lats, n, rows, cols, chans, pad, reach),
        out_shape=jax.ShapeDtypeStruct((rows, pad, chans), jnp.bfloat16),
        in_specs=[vmem] * 10,
        out_specs=vmem,
        scratch_shapes=[
            pltpu.VMEM((rows + 4, wide, full), jnp.float32),
            pltpu.VMEM((rows + 2, wide, chans), jnp.float32),
            pltpu.VMEM((rows, pad, chans), jnp.float32),
            pltpu.VMEM((rows, pad, chans), jnp.float32),
            pltpu.VMEM((rows, pad, chans), jnp.bfloat16),
            pltpu.VMEM((chunks, n + 2 * reach, pad, chans), jnp.bfloat16),
            pltpu.VMEM((rows, pad, chans), jnp.bfloat16),
            pltpu.VMEM((rows, pad, chans), jnp.bfloat16),
            pltpu.VMEM((2, rows + 4, 2, full), jnp.float32),
            pltpu.VMEM((chunks, pad, tap_lanes), jnp.bfloat16),
            sem((14,)), sem((14,)),
            sem((chunks, n)), sem((chunks, n)), sem((chunks, n)), sem((chunks, n)),
        ],
        compiler_params=pltpu.CompilerParams(
            collective_id=0, has_side_effects=True, vmem_limit_bytes=60 * 2**20
        ),
    )(
        inputs, spread, tb, lr, k_one, kernel_two, kept, norm_gain.reshape(1, chans),
        weight_in, weight_out,
    )
    return out[:, :cols]


def solution(mesh):
    placed = (
        P("lat", "lon", None),
        P("lat", "lon"),
        P(),
        P(),
        P("lat"),
        P("lat", None),
        P(),
        P(),
        P(),
    )
    return jax.shard_map(
        functools.partial(local, mesh.shape["lat"], mesh.shape["lon"]),
        mesh=mesh, in_specs=placed, out_specs=P("lat", "lon", None), check_vma=False,
    )
```

```python
import functools

import jax
import jax.numpy as jnp
from jax import lax
from jax.experimental import pallas as pl
from jax.experimental.pallas import tpu as pltpu
from jax.sharding import PartitionSpec as P

MESH = pl.DeviceIdType.MESH
LANES = 128
LEAD = 8


def round_up(value, step):
    return -(-value // step) * step


def gelu_tanh(values):
    return jax.nn.gelu(values, approximate=True)


def body(
    lats, n, rows, cols, chans, pad, reach,
    x_ref, metric_ref, k1_ref, k2_ref, widths_ref, gains_ref, gain_ref, win_hbm, wout_hbm,
    out_ref,
    ext, sec, held, acc, mix, circ, zsend, zrecv, lr_ref, side, taps, lines, taps_one, win_ref, wout_ref,
    w_sem,
    hs_sem, hr_sem, fs_sem, fr_sem, rs_sem, rr_sem,
):
    lat = lax.axis_index("lat")
    me = lax.axis_index("lon")
    chunks = rows // n
    half = n // 2
    wide = ext.shape[1]
    full = ext.shape[2]
    slabs = 2 * reach + 1

    at_top = lat == 0
    at_bottom = lat == lats - 1
    up_lat = jnp.where(at_top, 0, lat - 1)
    up_lon = jnp.where(at_top, lax.rem(me + half, n), me)
    down_lat = jnp.where(at_bottom, lats - 1, lat + 1)
    down_lon = jnp.where(at_bottom, lax.rem(me + half, n), me)
    left = lax.rem(me + n - 1, n)
    right = lax.rem(me + 1, n)

    def before(lon):
        return lax.rem(lon + n - 1, n)

    def after(lon):
        return lax.rem(lon + 1, n)

    loads = [
        pltpu.make_async_copy(win_hbm, win_ref, w_sem.at[0]),
        pltpu.make_async_copy(wout_hbm, wout_ref, w_sem.at[1]),
    ]
    for load in loads:
        load.start()

    barrier = pltpu.get_barrier_semaphore()
    greeted = [
        (lat, left), (lat, right),
        (up_lat, up_lon), (up_lat, before(up_lon)), (up_lat, after(up_lon)),
        (down_lat, down_lon), (down_lat, before(down_lon)), (down_lat, after(down_lon)),
    ] + [(lat, lax.rem(me + o, n)) for o in range(1, n)]
    for device in greeted:
        pl.semaphore_signal(barrier, inc=1, device_id=device, device_id_type=MESH)
    def clear(e, carry):
        ext[e, 0:LEAD, :] = jnp.zeros((LEAD, full), jnp.float32)
        return carry

    lax.fori_loop(0, rows + 4, clear, 0)

    diagonal = lax.broadcasted_iota(jnp.int32, (pad, cols), 0) == lax.broadcasted_iota(
        jnp.int32, (pad, cols), 1
    )

    def place(i, carry):
        line = jnp.broadcast_to(metric_ref[pl.ds(i, 1), :], (pad, cols))
        column = jnp.sum(jnp.where(diagonal, line, 0.0), axis=1, keepdims=True)
        weight = jnp.broadcast_to(column, (pad, LANES))
        ext[i + 2, pad:wide, :] = jnp.zeros((wide - pad, full), jnp.float32)
        held[i, pad - 8:pad, :] = jnp.zeros((8, chans), jnp.float32)
        ext[i + 2, LEAD:wide, chans:] = weight
        lr_ref[0, i, :, chans:] = weight[0:2]
        lr_ref[1, i, :, chans:] = weight[cols - 2:cols]
        for c in range(chans // LANES):
            lanes = slice(c * LANES, (c + 1) * LANES)
            cells = x_ref[i, :, lanes].astype(jnp.float32)
            held[i, 0:cols, lanes] = cells
            first = (cells * weight[0:cols]).astype(jnp.bfloat16).astype(jnp.float32)
            ext[i + 2, LEAD:LEAD + cols, lanes] = first
            lr_ref[0, i, :, lanes] = first[0:2]
            lr_ref[1, i, :, lanes] = first[cols - 2:cols]
        return carry

    lax.fori_loop(0, rows, place, 0)
    pl.semaphore_wait(barrier, len(greeted))

    halo = []

    def send_halo(src, dst, recv_index, device):
        copy = pltpu.make_async_remote_copy(
            src_ref=src, dst_ref=dst, send_sem=hs_sem.at[len(halo)], recv_sem=hr_sem.at[recv_index],
            device_id=device, device_id_type=MESH,
        )
        copy.start()
        halo.append(copy)

    def slot_row(slot):
        return jnp.where(slot < 2, slot, rows + slot)

    send_halo(lr_ref.at[0], side.at[1, pl.ds(2, rows)], 5, (lat, left))
    send_halo(lr_ref.at[1], side.at[0, pl.ds(2, rows)], 4, (lat, right))
    for i in range(2):
        up_slot = jnp.where(at_top, 1 - i, 2 + i)
        down_slot = jnp.where(at_bottom, 3 - i, i)
        for slot, src_row, device_lat, device_lon in (
            (up_slot, i, up_lat, up_lon),
            (down_slot, rows - 2 + i, down_lat, down_lon),
        ):
            dst_row = slot_row(slot)
            send_halo(
                ext.at[src_row + 2, pl.ds(LEAD, pad)], ext.at[dst_row, pl.ds(LEAD, pad)], slot, (device_lat, device_lon)
            )
            send_halo(
                lr_ref.at[0, src_row], side.at[1, dst_row], 10 + slot,
                (device_lat, before(device_lon)),
            )
            send_halo(
                lr_ref.at[1, src_row], side.at[0, dst_row], 6 + slot,
                (device_lat, after(device_lon)),
            )

    tap_lanes = taps.shape[2]
    lane_ids = lax.broadcasted_iota(jnp.int32, (pad, tap_lanes), 1)
    taps_one[0, 0:9] = k1_ref[...]
    for a in range(3):
        taps_one[1, 3 * a:3 * a + 3] = k1_ref[6 - 3 * a:9 - 3 * a, :]
    count = gains_ref.shape[1]
    center = (count - 1) // 2
    lines[...] = jnp.zeros(lines.shape, jnp.float32)
    lines[:, 0:count] = gains_ref[...].astype(jnp.float32)
    for k in range(chunks):
        line = jnp.broadcast_to(lines[pl.ds(k * n + me, 1), :], (pad, tap_lanes))
        kept = jnp.abs(lane_ids - center) <= widths_ref[k * n + me]
        line = jnp.where(kept, line, 0.0)
        shifted = pltpu.roll(line, 0, 1, stride=1, stride_axis=0)
        total = jnp.zeros((pad, tap_lanes), jnp.float32)
        for d in range(slabs):
            moved = pltpu.roll(shifted, (pad - cols) * d, 1) if d else shifted
            inside = (lane_ids >= pad * d) & (lane_ids < pad * d + cols)
            total = jnp.where(inside, moved, total)
        taps[k] = total.astype(jnp.bfloat16)

    def recv_halo(src, dst, recv_index):
        pltpu.make_async_remote_copy(
            src_ref=src, dst_ref=dst, send_sem=hs_sem.at[0], recv_sem=hr_sem.at[recv_index],
            device_id=(lat, right), device_id_type=MESH,
        ).wait_recv()

    for s in range(2):
        recv_halo(lr_ref.at[s], side.at[s, pl.ds(2, rows)], 4 + s)
    for slot in range(4):
        row = slot if slot < 2 else rows + slot
        recv_halo(ext.at[2, pl.ds(LEAD, pad)], ext.at[row, pl.ds(LEAD, pad)], slot)
        for s in range(2):
            recv_halo(lr_ref.at[0, 0], side.at[s, row], 6 + 4 * s + slot)

    for copy in halo:
        copy.wait_send()

    def join(e, carry):
        ext[e, LEAD - 2:LEAD, :] = side[0, e]
        ext[e, LEAD + cols:LEAD + cols + 2, :] = side[1, e]
        return carry

    lax.fori_loop(0, rows + 4, join, 0)

    def stencil(src, row, kernel, lanes):
        sums = [None, None, None]
        for a in range(3):
            line = src[row + a, :, lanes]
            for b in range(3):
                term = kernel(a, b, lanes) * line
                sums[b] = term if sums[b] is None else sums[b] + term
        return pltpu.roll(sums[0], 1, 0) + sums[1] + pltpu.roll(sums[2], wide - 1, 0)

    def second_row(p, carry):
        flip = ((p == 0) & at_top) | ((p == rows + 1) & at_bottom)
        which = jnp.where(flip, 1, 0)
        weight = ext[p + 1, :, chans:]
        for c in range(chans // LANES):
            lanes = slice(c * LANES, (c + 1) * LANES)
            value = stencil(ext, p, lambda a, b, l: taps_one[which, 3 * a + b:3 * a + b + 1, l], lanes)
            value = weight * gelu_tanh(value)
            sec[p, :, lanes] = value.astype(jnp.bfloat16).astype(jnp.float32)
        return carry

    col_ids = lax.broadcasted_iota(jnp.int32, (pad, LANES), 0)

    def mixed_row(i, carry):
        for c in range(chans // LANES):
            lanes = slice(c * LANES, (c + 1) * LANES)
            value = stencil(sec, i, lambda a, b, l: k2_ref[3 * a + b:3 * a + b + 1, l], lanes)
            value = held[i, :, lanes] + value[LEAD:, :]
            mix[i, :, lanes] = jnp.where(col_ids < cols, value, 0.0).astype(jnp.bfloat16)
        return carry

    forward = []
    for k in range(chunks):
        start = 0 if k == 0 else k * n + 2
        lax.fori_loop(start, (k + 1) * n + 2, second_row, 0)
        lax.fori_loop(k * n, (k + 1) * n, mixed_row, 0)
        for o in range(1, n):
            target = lax.rem(me + o, n)
            copy = pltpu.make_async_remote_copy(
                src_ref=mix.at[k * n + target], dst_ref=circ.at[k, me + reach],
                send_sem=fs_sem.at[k, o], recv_sem=fr_sem.at[k, o],
                device_id=(lat, target), device_id_type=MESH,
            )
            copy.start()
            forward.append(copy)
        circ[k, me + reach] = mix[k * n + me]

    for load in loads:
        load.wait()

    group = 8

    def network(g, carry):
        flat = mix[pl.ds(g * group, group)].reshape(group * pad, chans).astype(jnp.float32)
        scale = lax.rsqrt(jnp.mean(flat * flat, axis=1, keepdims=True) + 1e-06)
        normed = (flat * scale * gain_ref[...]).astype(jnp.bfloat16)
        hidden = gelu_tanh(
            jnp.dot(normed, win_ref[...], preferred_element_type=jnp.float32)
        ).astype(jnp.bfloat16)
        point = jnp.dot(hidden, wout_ref[...], preferred_element_type=jnp.float32)
        acc[pl.ds(g * group, group)] = (flat + point).reshape(group, pad, chans)
        return carry

    lax.fori_loop(0, rows // group, network, 0)

    back = []
    for k in range(chunks):
        for o in range(1, n):
            source = lax.rem(me + n - o, n)
            pltpu.make_async_remote_copy(
                src_ref=mix.at[k * n], dst_ref=circ.at[k, source + reach],
                send_sem=fs_sem.at[k, o], recv_sem=fr_sem.at[k, o],
                device_id=(lat, source), device_id_type=MESH,
            ).wait_recv()
        for e in range(reach):
            circ[k, e] = circ[k, n + e]
            circ[k, n + reach + e] = circ[k, reach + e]

        def filter_block(a, carry):
            window = circ[k, pl.ds(a, slabs)].reshape(slabs * pad, chans)
            result = jnp.dot(
                taps[k, :, 0:slabs * pad], window, preferred_element_type=jnp.float32
            )
            zsend[k * n + a] = result.astype(jnp.bfloat16)
            return carry

        lax.fori_loop(0, n, filter_block, 0, unroll=4)
        for o in range(1, n):
            target = lax.rem(me + o, n)
            copy = pltpu.make_async_remote_copy(
                src_ref=zsend.at[k * n + target], dst_ref=zrecv.at[k * n + me],
                send_sem=rs_sem.at[k, o], recv_sem=rr_sem.at[k, o],
                device_id=(lat, target), device_id_type=MESH,
            )
            copy.start()
            back.append(copy)
        zrecv[k * n + me] = zsend[k * n + me]

    for k in range(chunks):
        for o in range(1, n):
            source = lax.rem(me + n - o, n)
            pltpu.make_async_remote_copy(
                src_ref=zsend.at[k * n], dst_ref=zrecv.at[k * n + source],
                send_sem=rs_sem.at[k, o], recv_sem=rr_sem.at[k, o],
                device_id=(lat, source), device_id_type=MESH,
            ).wait_recv()

        def finish(i, carry):
            out_ref[i] = (acc[i] + zrecv[i].astype(jnp.float32)).astype(jnp.bfloat16)
            return carry

        lax.fori_loop(k * n, (k + 1) * n, finish, 0)

    for copy in forward + back:
        copy.wait_send()


def local(
    lats, n,
    inputs, metric, kernel_one, kernel_two, widths, zonal_gains, norm_gain, weight_in, weight_out
):
    rows, cols, chans = inputs.shape
    pad = round_up(cols, 16)
    wide = LEAD + pad
    full = chans + LANES
    reach = n // 4
    slabs = 2 * reach + 1
    count = zonal_gains.shape[1]
    tap_lanes = round_up(max(slabs * pad, count + pad - 1), LANES)

    chunks = rows // n
    vmem = pl.BlockSpec(memory_space=pltpu.VMEM)
    sem = pltpu.SemaphoreType.DMA
    out = pl.pallas_call(
        functools.partial(body, lats, n, rows, cols, chans, pad, reach),
        out_shape=jax.ShapeDtypeStruct((rows, pad, chans), jnp.bfloat16),
        in_specs=[vmem] * 4
        + [pl.BlockSpec(memory_space=pltpu.SMEM), vmem, vmem]
        + [pl.BlockSpec(memory_space=pl.ANY)] * 2,
        out_specs=vmem,
        scratch_shapes=[
            pltpu.VMEM((rows + 4, wide, full), jnp.float32),
            pltpu.VMEM((rows + 2, wide, chans), jnp.float32),
            pltpu.VMEM((rows, pad, chans), jnp.float32),
            pltpu.VMEM((rows, pad, chans), jnp.float32),
            pltpu.VMEM((rows, pad, chans), jnp.bfloat16),
            pltpu.VMEM((chunks, n + 2 * reach, pad, chans), jnp.bfloat16),
            pltpu.VMEM((rows, pad, chans), jnp.bfloat16),
            pltpu.VMEM((rows, pad, chans), jnp.bfloat16),
            pltpu.VMEM((2, rows, 2, full), jnp.float32),
            pltpu.VMEM((2, rows + 4, 2, full), jnp.float32),
            pltpu.VMEM((chunks, pad, tap_lanes), jnp.bfloat16),
            pltpu.VMEM((rows, tap_lanes), jnp.float32),
            pltpu.VMEM((2, 16, chans), jnp.float32),
            pltpu.VMEM(weight_in.shape, jnp.bfloat16),
            pltpu.VMEM(weight_out.shape, jnp.bfloat16),
            sem((2,)),
            sem((14,)), sem((14,)),
            sem((chunks, n)), sem((chunks, n)), sem((chunks, n)), sem((chunks, n)),
        ],
        compiler_params=pltpu.CompilerParams(
            collective_id=0, has_side_effects=True, vmem_limit_bytes=60 * 2**20
        ),
    )(
        inputs, metric, kernel_one, kernel_two, widths, zonal_gains, norm_gain.reshape(1, chans),
        weight_in, weight_out,
    )
    return out[:, :cols]


def solution(mesh):
    placed = (
        P("lat", "lon", None),
        P("lat", "lon"),
        P(),
        P(),
        P("lat"),
        P("lat", None),
        P(),
        P(),
        P(),
    )
    return jax.shard_map(
        functools.partial(local, mesh.shape["lat"], mesh.shape["lon"]),
        mesh=mesh, in_specs=placed, out_specs=P("lat", "lon", None), check_vma=False,
    )
```

```python
import functools

import jax
import jax.numpy as jnp
from jax import lax
from jax.experimental import pallas as pl
from jax.experimental.pallas import tpu as pltpu
from jax.sharding import PartitionSpec as P

MESH = pl.DeviceIdType.MESH
LANES = 128
LEAD = 8


def round_up(value, step):
    return -(-value // step) * step


def gelu_tanh(values):
    return jax.nn.gelu(values, approximate=True)


def body(
    lats, n, rows, cols, chans, pad, reach,
    x_ref, metric_ref, k1_ref, k2_ref, widths_ref, gains_ref, gain_ref, win_hbm, wout_hbm,
    out_ref,
    ext, sec, held, acc, mix, circ, zsend, zrecv, flatx, edge, edge_in, strip, strip_in, rim, rim_in,
    taps, lines, taps_one, win_ref, wout_ref,
    w_sem,
    hs_sem, hr_sem, fs_sem, fr_sem, rs_sem, rr_sem,
):
    lat = lax.axis_index("lat")
    me = lax.axis_index("lon")
    chunks = rows // n
    half = n // 2
    wide = ext.shape[1]
    full = ext.shape[2]
    slabs = 2 * reach + 1

    at_top = lat == 0
    at_bottom = lat == lats - 1
    up_lat = jnp.where(at_top, 0, lat - 1)
    up_lon = jnp.where(at_top, lax.rem(me + half, n), me)
    down_lat = jnp.where(at_bottom, lats - 1, lat + 1)
    down_lon = jnp.where(at_bottom, lax.rem(me + half, n), me)
    left = lax.rem(me + n - 1, n)
    right = lax.rem(me + 1, n)

    def before(lon):
        return lax.rem(lon + n - 1, n)

    def after(lon):
        return lax.rem(lon + 1, n)

    loads = [
        pltpu.make_async_copy(win_hbm, win_ref, w_sem.at[0]),
        pltpu.make_async_copy(wout_hbm, wout_ref, w_sem.at[1]),
    ]
    for load in loads:
        load.start()

    barrier = pltpu.get_barrier_semaphore()
    greeted = [
        (lat, left), (lat, right),
        (up_lat, up_lon), (up_lat, before(up_lon)), (up_lat, after(up_lon)),
        (down_lat, down_lon), (down_lat, before(down_lon)), (down_lat, after(down_lon)),
    ] + [(lat, lax.rem(me + o, n)) for o in range(1, n)]
    for device in greeted:
        pl.semaphore_signal(barrier, inc=1, device_id=device, device_id_type=MESH)
    def clear(e, carry):
        ext[e, 0:LEAD, :] = jnp.zeros((LEAD, full), jnp.float32)
        return carry

    lax.fori_loop(0, rows + 4, clear, 0)

    diagonal = lax.broadcasted_iota(jnp.int32, (pad, cols), 0) == lax.broadcasted_iota(
        jnp.int32, (pad, cols), 1
    )

    for c in range(chans // LANES):
        lanes = slice(c * LANES, (c + 1) * LANES)
        flatx[c] = x_ref[:, :, lanes].astype(jnp.float32).reshape(cols * rows, LANES)

    def place(i, carry):
        line = jnp.broadcast_to(metric_ref[pl.ds(i, 1), :], (pad, cols))
        column = jnp.sum(jnp.where(diagonal, line, 0.0), axis=1, keepdims=True)
        weight = jnp.broadcast_to(column, (pad, LANES))
        ext[i + 2, pad:wide, :] = jnp.zeros((wide - pad, full), jnp.float32)
        held[i, pad - 8:pad, :] = jnp.zeros((8, chans), jnp.float32)
        ext[i + 2, LEAD:wide, chans:] = weight
        rim[0, i] = weight[0:1]
        rim[1, i] = weight[cols - 1:cols]
        for c in range(chans // LANES):
            lanes = slice(c * LANES, (c + 1) * LANES)
            cells = flatx[c, pl.ds(i, cols, stride=rows), :]
            held[i, 0:cols, lanes] = cells
            first = (cells * weight[0:cols]).astype(jnp.bfloat16).astype(jnp.float32)
            ext[i + 2, LEAD:LEAD + cols, lanes] = first
            strip[0, i, :, lanes] = first[0:2].astype(jnp.bfloat16)
            strip[1, i, :, lanes] = first[cols - 2:cols].astype(jnp.bfloat16)
        return carry

    lax.fori_loop(0, rows, place, 0)
    for slot, row in enumerate((2, 3, rows, rows + 1)):
        edge[slot] = ext[row, LEAD:wide, 0:chans].astype(jnp.bfloat16)
    pl.semaphore_wait(barrier, len(greeted))

    halo = []

    def send_halo(src, dst, recv_index, device):
        copy = pltpu.make_async_remote_copy(
            src_ref=src, dst_ref=dst, send_sem=hs_sem.at[len(halo)], recv_sem=hr_sem.at[recv_index],
            device_id=device, device_id_type=MESH,
        )
        copy.start()
        halo.append(copy)

    def slot_row(slot):
        return jnp.where(slot < 2, slot, rows + slot)

    for s, device in ((0, left), (1, right)):
        send_halo(strip.at[s], strip_in.at[1 - s, pl.ds(2, rows)], 4 + s, (lat, device))
        send_halo(rim.at[s], rim_in.at[1 - s, pl.ds(2, rows)], 6 + s, (lat, device))
    for i in range(2):
        up_slot = jnp.where(at_top, 1 - i, 2 + i)
        down_slot = jnp.where(at_bottom, 3 - i, i)
        for slot, src_row, device_lat, device_lon in (
            (up_slot, i, up_lat, up_lon),
            (down_slot, rows - 2 + i, down_lat, down_lon),
        ):
            source = i if src_row < 2 else 2 + i
            dst_row = slot_row(slot)
            target = (device_lat, device_lon)
            send_halo(edge.at[source], edge_in.at[slot], slot, target)
            corners = ((0, before(device_lon)), (1, after(device_lon)))
            for s, corner_lon in corners:
                send_halo(
                    strip.at[s, src_row], strip_in.at[1 - s, dst_row], 8 + 4 * s + slot,
                    (device_lat, corner_lon),
                )
            if src_row in (0, rows - 1):
                near = jnp.where(slot < 2, 0, 1)
                send_halo(
                    ext.at[src_row + 2, pl.ds(LEAD, pad), pl.ds(chans, LANES)],
                    ext.at[dst_row, pl.ds(LEAD, pad), pl.ds(chans, LANES)],
                    16 + near, target,
                )
                for s, corner_lon in corners:
                    send_halo(
                        rim.at[s, src_row], rim_in.at[1 - s, dst_row], 18 + 2 * s + near,
                        (device_lat, corner_lon),
                    )

    tap_lanes = taps.shape[2]
    lane_ids = lax.broadcasted_iota(jnp.int32, (pad, tap_lanes), 1)
    taps_one[0, 0:9] = k1_ref[...]
    for a in range(3):
        taps_one[1, 3 * a:3 * a + 3] = k1_ref[6 - 3 * a:9 - 3 * a, :]
    count = gains_ref.shape[1]
    center = (count - 1) // 2
    lines[...] = jnp.zeros(lines.shape, jnp.float32)
    lines[:, 0:count] = gains_ref[...].astype(jnp.float32)
    for k in range(chunks):
        line = jnp.broadcast_to(lines[pl.ds(k * n + me, 1), :], (pad, tap_lanes))
        kept = jnp.abs(lane_ids - center) <= widths_ref[k * n + me]
        line = jnp.where(kept, line, 0.0)
        shifted = pltpu.roll(line, 0, 1, stride=1, stride_axis=0)
        total = jnp.zeros((pad, tap_lanes), jnp.float32)
        for d in range(slabs):
            moved = pltpu.roll(shifted, (pad - cols) * d, 1) if d else shifted
            inside = (lane_ids >= pad * d) & (lane_ids < pad * d + cols)
            total = jnp.where(inside, moved, total)
        taps[k] = total.astype(jnp.bfloat16)

    def recv_halo(src, dst, recv_index):
        pltpu.make_async_remote_copy(
            src_ref=src, dst_ref=dst, send_sem=hs_sem.at[0], recv_sem=hr_sem.at[recv_index],
            device_id=(lat, right), device_id_type=MESH,
        ).wait_recv()

    for s in range(2):
        recv_halo(strip.at[s], strip_in.at[1 - s, pl.ds(2, rows)], 4 + s)
        recv_halo(rim.at[s], rim_in.at[1 - s, pl.ds(2, rows)], 6 + s)
        row = (1, rows + 2)[s]
        recv_halo(
            ext.at[2, pl.ds(LEAD, pad), pl.ds(chans, LANES)],
            ext.at[row, pl.ds(LEAD, pad), pl.ds(chans, LANES)], 16 + s,
        )
        for near in range(2):
            recv_halo(rim.at[s, 0], rim_in.at[1 - s, (1, rows + 2)[near]], 18 + 2 * s + near)
    for slot in range(4):
        row = slot if slot < 2 else rows + slot
        recv_halo(edge.at[0], edge_in.at[slot], slot)
        for s in range(2):
            recv_halo(strip.at[s, 0], strip_in.at[1 - s, row], 8 + 4 * s + slot)
    for copy in halo:
        copy.wait_send()

    for slot in range(4):
        row = slot if slot < 2 else rows + slot
        ext[row, LEAD:wide, 0:chans] = edge_in[slot].astype(jnp.float32)

    def join(e, carry):
        for s, at in ((0, LEAD - 2), (1, LEAD + cols)):
            ext[e, at:at + 2, 0:chans] = strip_in[s, e].astype(jnp.float32)
        return carry

    def join_rim(e, carry):
        ext[e, LEAD - 1:LEAD, chans:] = rim_in[0, e]
        ext[e, LEAD + cols:LEAD + cols + 1, chans:] = rim_in[1, e]
        return carry

    lax.fori_loop(1, rows + 3, join_rim, 0)
    lax.fori_loop(0, rows + 4, join, 0)

    def stencil(src, row, kernel, lanes):
        sums = [None, None, None]
        for a in range(3):
            line = src[row + a, :, lanes]
            for b in range(3):
                term = kernel(a, b, lanes) * line
                sums[b] = term if sums[b] is None else sums[b] + term
        return pltpu.roll(sums[0], 1, 0) + sums[1] + pltpu.roll(sums[2], wide - 1, 0)

    def second_row(p, carry):
        flip = ((p == 0) & at_top) | ((p == rows + 1) & at_bottom)
        which = jnp.where(flip, 1, 0)
        weight = ext[p + 1, :, chans:]
        for c in range(chans // LANES):
            lanes = slice(c * LANES, (c + 1) * LANES)
            value = stencil(ext, p, lambda a, b, l: taps_one[which, 3 * a + b:3 * a + b + 1, l], lanes)
            value = weight * gelu_tanh(value)
            sec[p, :, lanes] = value.astype(jnp.bfloat16).astype(jnp.float32)
        return carry

    col_ids = lax.broadcasted_iota(jnp.int32, (pad, LANES), 0)

    def mixed_row(i, carry):
        for c in range(chans // LANES):
            lanes = slice(c * LANES, (c + 1) * LANES)
            value = stencil(sec, i, lambda a, b, l: k2_ref[3 * a + b:3 * a + b + 1, l], lanes)
            value = held[i, :, lanes] + value[LEAD:, :]
            mix[i, :, lanes] = jnp.where(col_ids < cols, value, 0.0).astype(jnp.bfloat16)
        return carry

    forward = []
    for k in range(chunks):
        start = 0 if k == 0 else k * n + 2
        lax.fori_loop(start, (k + 1) * n + 2, second_row, 0)
        lax.fori_loop(k * n, (k + 1) * n, mixed_row, 0)
        for o in range(1, n):
            target = lax.rem(me + o, n)
            copy = pltpu.make_async_remote_copy(
                src_ref=mix.at[k * n + target], dst_ref=circ.at[k, me + reach],
                send_sem=fs_sem.at[k, o], recv_sem=fr_sem.at[k, o],
                device_id=(lat, target), device_id_type=MESH,
            )
            copy.start()
            forward.append(copy)
        circ[k, me + reach] = mix[k * n + me]

    for load in loads:
        load.wait()

    group = 8

    def network(g, carry):
        flat = mix[pl.ds(g * group, group)].reshape(group * pad, chans).astype(jnp.float32)
        scale = lax.rsqrt(jnp.mean(flat * flat, axis=1, keepdims=True) + 1e-06)
        normed = (flat * scale * gain_ref[...]).astype(jnp.bfloat16)
        hidden = gelu_tanh(
            jnp.dot(normed, win_ref[...], preferred_element_type=jnp.float32)
        ).astype(jnp.bfloat16)
        point = jnp.dot(hidden, wout_ref[...], preferred_element_type=jnp.float32)
        acc[pl.ds(g * group, group)] = (flat + point).reshape(group, pad, chans)
        return carry

    lax.fori_loop(0, rows // group, network, 0)

    back = []
    for k in range(chunks):
        for o in range(1, n):
            source = lax.rem(me + n - o, n)
            pltpu.make_async_remote_copy(
                src_ref=mix.at[k * n], dst_ref=circ.at[k, source + reach],
                send_sem=fs_sem.at[k, o], recv_sem=fr_sem.at[k, o],
                device_id=(lat, source), device_id_type=MESH,
            ).wait_recv()
        for e in range(reach):
            circ[k, e] = circ[k, n + e]
            circ[k, n + reach + e] = circ[k, reach + e]

        def filter_block(a, carry):
            window = circ[k, pl.ds(a, slabs)].reshape(slabs * pad, chans)
            result = jnp.dot(
                taps[k, :, 0:slabs * pad], window, preferred_element_type=jnp.float32
            )
            zsend[k * n + a] = result.astype(jnp.bfloat16)
            return carry

        lax.fori_loop(0, n, filter_block, 0, unroll=4)
        for o in range(1, n):
            target = lax.rem(me + o, n)
            copy = pltpu.make_async_remote_copy(
                src_ref=zsend.at[k * n + target], dst_ref=zrecv.at[k * n + me],
                send_sem=rs_sem.at[k, o], recv_sem=rr_sem.at[k, o],
                device_id=(lat, target), device_id_type=MESH,
            )
            copy.start()
            back.append(copy)
        zrecv[k * n + me] = zsend[k * n + me]

    for k in range(chunks):
        for o in range(1, n):
            source = lax.rem(me + n - o, n)
            pltpu.make_async_remote_copy(
                src_ref=zsend.at[k * n], dst_ref=zrecv.at[k * n + source],
                send_sem=rs_sem.at[k, o], recv_sem=rr_sem.at[k, o],
                device_id=(lat, source), device_id_type=MESH,
            ).wait_recv()

        def finish(i, carry):
            out_ref[i] = (acc[i] + zrecv[i].astype(jnp.float32)).astype(jnp.bfloat16)
            return carry

        lax.fori_loop(k * n, (k + 1) * n, finish, 0)

    for copy in forward + back:
        copy.wait_send()


def local(
    lats, n,
    inputs, metric, kernel_one, kernel_two, widths, zonal_gains, norm_gain, weight_in, weight_out
):
    rows, cols, chans = inputs.shape
    pad = round_up(cols, 16)
    wide = LEAD + pad
    full = chans + LANES
    reach = n // 4
    slabs = 2 * reach + 1
    count = zonal_gains.shape[1]
    tap_lanes = round_up(max(slabs * pad, count + pad - 1), LANES)

    chunks = rows // n
    vmem = pl.BlockSpec(memory_space=pltpu.VMEM)
    sem = pltpu.SemaphoreType.DMA
    out = pl.pallas_call(
        functools.partial(body, lats, n, rows, cols, chans, pad, reach),
        out_shape=jax.ShapeDtypeStruct((rows, pad, chans), jnp.bfloat16),
        in_specs=[vmem] * 4
        + [pl.BlockSpec(memory_space=pltpu.SMEM), vmem, vmem]
        + [pl.BlockSpec(memory_space=pl.ANY)] * 2,
        out_specs=vmem,
        scratch_shapes=[
            pltpu.VMEM((rows + 4, wide, full), jnp.float32),
            pltpu.VMEM((rows + 2, wide, chans), jnp.float32),
            pltpu.VMEM((rows, pad, chans), jnp.float32),
            pltpu.VMEM((rows, pad, chans), jnp.float32),
            pltpu.VMEM((rows, pad, chans), jnp.bfloat16),
            pltpu.VMEM((chunks, n + 2 * reach, pad, chans), jnp.bfloat16),
            pltpu.VMEM((rows, pad, chans), jnp.bfloat16),
            pltpu.VMEM((rows, pad, chans), jnp.bfloat16),
            pltpu.VMEM((chans // LANES, cols * rows, LANES), jnp.float32),
            pltpu.VMEM((4, pad, chans), jnp.bfloat16),
            pltpu.VMEM((4, pad, chans), jnp.bfloat16),
            pltpu.VMEM((2, rows, 2, chans), jnp.bfloat16),
            pltpu.VMEM((2, rows + 4, 2, chans), jnp.bfloat16),
            pltpu.VMEM((2, rows, 1, LANES), jnp.float32),
            pltpu.VMEM((2, rows + 4, 1, LANES), jnp.float32),
            pltpu.VMEM((chunks, pad, tap_lanes), jnp.bfloat16),
            pltpu.VMEM((rows, tap_lanes), jnp.float32),
            pltpu.VMEM((2, 16, chans), jnp.float32),
            pltpu.VMEM(weight_in.shape, jnp.bfloat16),
            pltpu.VMEM(weight_out.shape, jnp.bfloat16),
            sem((2,)),
            sem((22,)), sem((22,)),
            sem((chunks, n)), sem((chunks, n)), sem((chunks, n)), sem((chunks, n)),
        ],
        compiler_params=pltpu.CompilerParams(
            collective_id=0, has_side_effects=True, vmem_limit_bytes=60 * 2**20
        ),
    )(
        inputs.transpose(1, 0, 2), metric, kernel_one, kernel_two, widths, zonal_gains, norm_gain.reshape(1, chans),
        weight_in, weight_out,
    )
    return out[:, :cols]


def solution(mesh):
    placed = (
        P("lat", "lon", None),
        P("lat", "lon"),
        P(),
        P(),
        P("lat"),
        P("lat", None),
        P(),
        P(),
        P(),
    )
    return jax.shard_map(
        functools.partial(local, mesh.shape["lat"], mesh.shape["lon"]),
        mesh=mesh, in_specs=placed, out_specs=P("lat", "lon", None), check_vma=False,
    )
```

```python
import functools

import jax
import jax.numpy as jnp
from jax import lax
from jax.experimental import pallas as pl
from jax.experimental.pallas import tpu as pltpu
from jax.sharding import PartitionSpec as P

MESH = pl.DeviceIdType.MESH
LANES = 128
LEAD = 8


def round_up(value, step):
    return -(-value // step) * step


def gelu_tanh(values):
    return jax.nn.gelu(values, approximate=True)


def body(
    lats, n, rows, cols, chans, pad, reach,
    x_ref, metric_ref, k1_ref, k2_ref, widths_ref, gains_ref, gain_ref, win_hbm, wout_hbm,
    out_ref,
    ext, sec, held, acc, mix, circ, zsend, zrecv, flatx, edge, edge_in, strip, strip_in, rim, rim_in,
    taps, lines, taps_one, win_ref, wout_ref,
    w_sem,
    hs_sem, hr_sem, fs_sem, fr_sem, rs_sem, rr_sem,
):
    lat = lax.axis_index("lat")
    me = lax.axis_index("lon")
    chunks = rows // n
    half = n // 2
    wide = ext.shape[1]
    full = ext.shape[2]
    slabs = 2 * reach + 1

    at_top = lat == 0
    at_bottom = lat == lats - 1
    up_lat = jnp.where(at_top, 0, lat - 1)
    up_lon = jnp.where(at_top, lax.rem(me + half, n), me)
    down_lat = jnp.where(at_bottom, lats - 1, lat + 1)
    down_lon = jnp.where(at_bottom, lax.rem(me + half, n), me)
    left = lax.rem(me + n - 1, n)
    right = lax.rem(me + 1, n)

    def before(lon):
        return lax.rem(lon + n - 1, n)

    def after(lon):
        return lax.rem(lon + 1, n)

    loads = [
        pltpu.make_async_copy(win_hbm, win_ref, w_sem.at[0]),
        pltpu.make_async_copy(wout_hbm, wout_ref, w_sem.at[1]),
    ]
    for load in loads:
        load.start()

    barrier = pltpu.get_barrier_semaphore()
    greeted = [
        (lat, left), (lat, right),
        (up_lat, up_lon), (up_lat, before(up_lon)), (up_lat, after(up_lon)),
        (down_lat, down_lon), (down_lat, before(down_lon)), (down_lat, after(down_lon)),
    ] + [(lat, lax.rem(me + o, n)) for o in range(1, n)]
    for device in greeted:
        pl.semaphore_signal(barrier, inc=1, device_id=device, device_id_type=MESH)
    def clear(e, carry):
        ext[e, 0:LEAD, :] = jnp.zeros((LEAD, full), jnp.float32)
        return carry

    lax.fori_loop(0, rows + 4, clear, 0)

    diagonal = lax.broadcasted_iota(jnp.int32, (pad, cols), 0) == lax.broadcasted_iota(
        jnp.int32, (pad, cols), 1
    )

    for c in range(chans // LANES):
        lanes = slice(c * LANES, (c + 1) * LANES)
        flatx[c] = x_ref[:, :, lanes].astype(jnp.float32).reshape(cols * rows, LANES)

    def place(i, carry):
        line = jnp.broadcast_to(metric_ref[pl.ds(i, 1), :], (pad, cols))
        column = jnp.sum(jnp.where(diagonal, line, 0.0), axis=1, keepdims=True)
        weight = jnp.broadcast_to(column, (pad, LANES))
        ext[i + 2, pad:wide, :] = jnp.zeros((wide - pad, full), jnp.float32)
        held[i, pad - 8:pad, :] = jnp.zeros((8, chans), jnp.float32)
        ext[i + 2, LEAD:wide, chans:] = weight
        rim[0, i] = weight[0:1]
        rim[1, i] = weight[cols - 1:cols]
        for c in range(chans // LANES):
            lanes = slice(c * LANES, (c + 1) * LANES)
            cells = flatx[c, pl.ds(i, cols, stride=rows), :]
            held[i, 0:cols, lanes] = cells
            first = (cells * weight[0:cols]).astype(jnp.bfloat16).astype(jnp.float32)
            ext[i + 2, LEAD:LEAD + cols, lanes] = first
            strip[0, i, :, lanes] = first[0:2].astype(jnp.bfloat16)
            strip[1, i, :, lanes] = first[cols - 2:cols].astype(jnp.bfloat16)
        return carry

    lax.fori_loop(0, rows, place, 0)
    for slot, row in enumerate((2, 3, rows, rows + 1)):
        edge[slot] = ext[row, LEAD:wide, 0:chans].astype(jnp.bfloat16)
    pl.semaphore_wait(barrier, len(greeted))

    halo = []

    def send_halo(src, dst, recv_index, device):
        copy = pltpu.make_async_remote_copy(
            src_ref=src, dst_ref=dst, send_sem=hs_sem.at[len(halo)], recv_sem=hr_sem.at[recv_index],
            device_id=device, device_id_type=MESH,
        )
        copy.start()
        halo.append(copy)

    def slot_row(slot):
        return jnp.where(slot < 2, slot, rows + slot)

    for s, device in ((0, left), (1, right)):
        send_halo(strip.at[s], strip_in.at[1 - s, pl.ds(2, rows)], 4 + s, (lat, device))
        send_halo(rim.at[s], rim_in.at[1 - s, pl.ds(2, rows)], 6 + s, (lat, device))
    for i in range(2):
        up_slot = jnp.where(at_top, 1 - i, 2 + i)
        down_slot = jnp.where(at_bottom, 3 - i, i)
        for slot, src_row, device_lat, device_lon in (
            (up_slot, i, up_lat, up_lon),
            (down_slot, rows - 2 + i, down_lat, down_lon),
        ):
            source = i if src_row < 2 else 2 + i
            dst_row = slot_row(slot)
            target = (device_lat, device_lon)
            send_halo(edge.at[source], edge_in.at[slot], slot, target)
            corners = ((0, before(device_lon)), (1, after(device_lon)))
            for s, corner_lon in corners:
                send_halo(
                    strip.at[s, src_row], strip_in.at[1 - s, dst_row], 8 + 4 * s + slot,
                    (device_lat, corner_lon),
                )
            if src_row in (0, rows - 1):
                near = jnp.where(slot < 2, 0, 1)
                send_halo(
                    ext.at[src_row + 2, pl.ds(LEAD, pad), pl.ds(chans, LANES)],
                    ext.at[dst_row, pl.ds(LEAD, pad), pl.ds(chans, LANES)],
                    16 + near, target,
                )
                for s, corner_lon in corners:
                    send_halo(
                        rim.at[s, src_row], rim_in.at[1 - s, dst_row], 18 + 2 * s + near,
                        (device_lat, corner_lon),
                    )

    tap_lanes = taps.shape[2]
    lane_ids = lax.broadcasted_iota(jnp.int32, (pad, tap_lanes), 1)
    taps_one[0, 0:9] = k1_ref[...]
    for a in range(3):
        taps_one[1, 3 * a:3 * a + 3] = k1_ref[6 - 3 * a:9 - 3 * a, :]
    count = gains_ref.shape[1]
    center = (count - 1) // 2
    lines[...] = jnp.zeros(lines.shape, jnp.float32)
    lines[:, 0:count] = gains_ref[...].astype(jnp.float32)
    for k in range(chunks):
        line = jnp.broadcast_to(lines[pl.ds(k * n + me, 1), :], (pad, tap_lanes))
        kept = jnp.abs(lane_ids - center) <= widths_ref[k * n + me]
        line = jnp.where(kept, line, 0.0)
        shifted = pltpu.roll(line, 0, 1, stride=1, stride_axis=0)
        total = jnp.zeros((pad, tap_lanes), jnp.float32)
        for d in range(slabs):
            moved = pltpu.roll(shifted, (pad - cols) * d, 1) if d else shifted
            inside = (lane_ids >= pad * d) & (lane_ids < pad * d + cols)
            total = jnp.where(inside, moved, total)
        taps[k] = total.astype(jnp.bfloat16)

    def recv_halo(src, dst, recv_index):
        pltpu.make_async_remote_copy(
            src_ref=src, dst_ref=dst, send_sem=hs_sem.at[0], recv_sem=hr_sem.at[recv_index],
            device_id=(lat, right), device_id_type=MESH,
        ).wait_recv()

    for s in range(2):
        recv_halo(strip.at[s], strip_in.at[1 - s, pl.ds(2, rows)], 4 + s)
        recv_halo(rim.at[s], rim_in.at[1 - s, pl.ds(2, rows)], 6 + s)
        row = (1, rows + 2)[s]
        recv_halo(
            ext.at[2, pl.ds(LEAD, pad), pl.ds(chans, LANES)],
            ext.at[row, pl.ds(LEAD, pad), pl.ds(chans, LANES)], 16 + s,
        )
        for near in range(2):
            recv_halo(rim.at[s, 0], rim_in.at[1 - s, (1, rows + 2)[near]], 18 + 2 * s + near)
    for slot in range(4):
        row = slot if slot < 2 else rows + slot
        recv_halo(edge.at[0], edge_in.at[slot], slot)
        for s in range(2):
            recv_halo(strip.at[s, 0], strip_in.at[1 - s, row], 8 + 4 * s + slot)
    for copy in halo:
        copy.wait_send()

    for slot in range(4):
        row = slot if slot < 2 else rows + slot
        ext[row, LEAD:wide, 0:chans] = edge_in[slot].astype(jnp.float32)

    def join(e, carry):
        for s, at in ((0, LEAD - 2), (1, LEAD + cols)):
            ext[e, at:at + 2, 0:chans] = strip_in[s, e].astype(jnp.float32)
        return carry

    def join_rim(e, carry):
        ext[e, LEAD - 1:LEAD, chans:] = rim_in[0, e]
        ext[e, LEAD + cols:LEAD + cols + 1, chans:] = rim_in[1, e]
        return carry

    lax.fori_loop(1, rows + 3, join_rim, 0)
    lax.fori_loop(0, rows + 4, join, 0)

    def stencil(src, row, kernel, lanes):
        sums = [None, None, None]
        for a in range(3):
            line = src[row + a, :, lanes]
            for b in range(3):
                term = kernel(a, b, lanes) * line
                sums[b] = term if sums[b] is None else sums[b] + term
        return pltpu.roll(sums[0], 1, 0) + sums[1] + pltpu.roll(sums[2], wide - 1, 0)

    def second_row(p, carry):
        flip = ((p == 0) & at_top) | ((p == rows + 1) & at_bottom)
        which = jnp.where(flip, 1, 0)
        weight = ext[p + 1, :, chans:]
        for c in range(chans // LANES):
            lanes = slice(c * LANES, (c + 1) * LANES)
            value = stencil(ext, p, lambda a, b, l: taps_one[which, 3 * a + b:3 * a + b + 1, l], lanes)
            value = weight * gelu_tanh(value)
            sec[p, :, lanes] = value.astype(jnp.bfloat16).astype(jnp.float32)
        return carry

    col_ids = lax.broadcasted_iota(jnp.int32, (pad, LANES), 0)

    def mixed_row(i, carry):
        for c in range(chans // LANES):
            lanes = slice(c * LANES, (c + 1) * LANES)
            value = stencil(sec, i, lambda a, b, l: k2_ref[3 * a + b:3 * a + b + 1, l], lanes)
            value = held[i, :, lanes] + value[LEAD:, :]
            mix[i, :, lanes] = jnp.where(col_ids < cols, value, 0.0).astype(jnp.bfloat16)
        return carry

    forward = []
    for k in range(chunks):
        start = 0 if k == 0 else k * n + 2
        lax.fori_loop(start, (k + 1) * n + 2, second_row, 0)
        lax.fori_loop(k * n, (k + 1) * n, mixed_row, 0)
        for o in range(1, n):
            target = lax.rem(me + o, n)
            copy = pltpu.make_async_remote_copy(
                src_ref=mix.at[k * n + target], dst_ref=circ.at[k, me + reach],
                send_sem=fs_sem.at[k, o], recv_sem=fr_sem.at[k, o],
                device_id=(lat, target), device_id_type=MESH,
            )
            copy.start()
            forward.append(copy)
        circ[k, me + reach] = mix[k * n + me]

    for load in loads:
        load.wait()

    group = 8

    def network(g, carry):
        flat = mix[pl.ds(g * group, group)].reshape(group * pad, chans).astype(jnp.float32)
        scale = lax.rsqrt(jnp.mean(flat * flat, axis=1, keepdims=True) + 1e-06)
        normed = (flat * scale * gain_ref[...]).astype(jnp.bfloat16)
        hidden = gelu_tanh(
            jnp.dot(normed, win_ref[...], preferred_element_type=jnp.float32)
        ).astype(jnp.bfloat16)
        point = jnp.dot(hidden, wout_ref[...], preferred_element_type=jnp.float32)
        acc[pl.ds(g * group, group)] = (flat + point).reshape(group, pad, chans)
        return carry

    lax.fori_loop(0, rows // group, network, 0)

    back = []
    for k in range(chunks):
        for o in range(1, n):
            source = lax.rem(me + n - o, n)
            pltpu.make_async_remote_copy(
                src_ref=mix.at[k * n], dst_ref=circ.at[k, source + reach],
                send_sem=fs_sem.at[k, o], recv_sem=fr_sem.at[k, o],
                device_id=(lat, source), device_id_type=MESH,
            ).wait_recv()
        for e in range(reach):
            circ[k, e] = circ[k, n + e]
            circ[k, n + reach + e] = circ[k, reach + e]

        def filter_block(a, carry):
            window = circ[k, pl.ds(a, slabs)].reshape(slabs * pad, chans)
            result = jnp.dot(
                taps[k, :, 0:slabs * pad], window, preferred_element_type=jnp.float32
            )
            zsend[k * n + a] = result.astype(jnp.bfloat16)
            return carry

        lax.fori_loop(0, n, filter_block, 0, unroll=4)
        for o in range(1, n):
            target = lax.rem(me + o, n)
            copy = pltpu.make_async_remote_copy(
                src_ref=zsend.at[k * n + target], dst_ref=zrecv.at[k * n + me],
                send_sem=rs_sem.at[k, o], recv_sem=rr_sem.at[k, o],
                device_id=(lat, target), device_id_type=MESH,
            )
            copy.start()
            back.append(copy)
        zrecv[k * n + me] = zsend[k * n + me]

    done = 0
    for k in range(chunks):
        for o in range(1, n):
            source = lax.rem(me + n - o, n)
            pltpu.make_async_remote_copy(
                src_ref=zsend.at[k * n], dst_ref=zrecv.at[k * n + source],
                send_sem=rs_sem.at[k, o], recv_sem=rr_sem.at[k, o],
                device_id=(lat, source), device_id_type=MESH,
            ).wait_recv()

        def finish(i, carry):
            for c in range(chans // LANES):
                lanes = slice(c * LANES, (c + 1) * LANES)
                cells = acc[i, :, lanes] + zrecv[i, :, lanes].astype(jnp.float32)
                flatx[c, pl.ds(i, cols, stride=rows), :] = cells[0:cols]
            return carry

        lax.fori_loop(k * n, (k + 1) * n, finish, 0)
        low = done
        done = (k + 1) * n // 16 * 16
        if done > low:
            for c in range(chans // LANES):
                lanes = slice(c * LANES, (c + 1) * LANES)
                block = flatx[c].reshape(cols, rows, LANES)[:, low:done]
                out_ref[:, low:done, lanes] = block.astype(jnp.bfloat16)

    for copy in forward + back:
        copy.wait_send()


def local(
    lats, n,
    inputs, metric, kernel_one, kernel_two, widths, zonal_gains, norm_gain, weight_in, weight_out
):
    rows, cols, chans = inputs.shape
    pad = round_up(cols, 16)
    wide = LEAD + pad
    full = chans + LANES
    reach = n // 4
    slabs = 2 * reach + 1
    count = zonal_gains.shape[1]
    tap_lanes = round_up(max(slabs * pad, count + pad - 1), LANES)

    chunks = rows // n
    vmem = pl.BlockSpec(memory_space=pltpu.VMEM)
    sem = pltpu.SemaphoreType.DMA
    out = pl.pallas_call(
        functools.partial(body, lats, n, rows, cols, chans, pad, reach),
        out_shape=jax.ShapeDtypeStruct((cols, rows, chans), jnp.bfloat16),
        in_specs=[vmem] * 4
        + [pl.BlockSpec(memory_space=pltpu.SMEM), vmem, vmem]
        + [pl.BlockSpec(memory_space=pl.ANY)] * 2,
        out_specs=vmem,
        scratch_shapes=[
            pltpu.VMEM((rows + 4, wide, full), jnp.float32),
            pltpu.VMEM((rows + 2, wide, chans), jnp.float32),
            pltpu.VMEM((rows, pad, chans), jnp.float32),
            pltpu.VMEM((rows, pad, chans), jnp.float32),
            pltpu.VMEM((rows, pad, chans), jnp.bfloat16),
            pltpu.VMEM((chunks, n + 2 * reach, pad, chans), jnp.bfloat16),
            pltpu.VMEM((rows, pad, chans), jnp.bfloat16),
            pltpu.VMEM((rows, pad, chans), jnp.bfloat16),
            pltpu.VMEM((chans // LANES, cols * rows, LANES), jnp.float32),
            pltpu.VMEM((4, pad, chans), jnp.bfloat16),
            pltpu.VMEM((4, pad, chans), jnp.bfloat16),
            pltpu.VMEM((2, rows, 2, chans), jnp.bfloat16),
            pltpu.VMEM((2, rows + 4, 2, chans), jnp.bfloat16),
            pltpu.VMEM((2, rows, 1, LANES), jnp.float32),
            pltpu.VMEM((2, rows + 4, 1, LANES), jnp.float32),
            pltpu.VMEM((chunks, pad, tap_lanes), jnp.bfloat16),
            pltpu.VMEM((rows, tap_lanes), jnp.float32),
            pltpu.VMEM((2, 16, chans), jnp.float32),
            pltpu.VMEM(weight_in.shape, jnp.bfloat16),
            pltpu.VMEM(weight_out.shape, jnp.bfloat16),
            sem((2,)),
            sem((22,)), sem((22,)),
            sem((chunks, n)), sem((chunks, n)), sem((chunks, n)), sem((chunks, n)),
        ],
        compiler_params=pltpu.CompilerParams(
            collective_id=0, has_side_effects=True, vmem_limit_bytes=60 * 2**20
        ),
    )(
        inputs.transpose(1, 0, 2), metric, kernel_one, kernel_two, widths, zonal_gains, norm_gain.reshape(1, chans),
        weight_in, weight_out,
    )
    return out.transpose(1, 0, 2)


def solution(mesh):
    placed = (
        P("lat", "lon", None),
        P("lat", "lon"),
        P(),
        P(),
        P("lat"),
        P("lat", None),
        P(),
        P(),
        P(),
    )
    return jax.shard_map(
        functools.partial(local, mesh.shape["lat"], mesh.shape["lon"]),
        mesh=mesh, in_specs=placed, out_specs=P("lat", "lon", None), check_vma=False,
    )
```

```python
import functools

import jax
import jax.numpy as jnp
from jax import lax
from jax.experimental import pallas as pl
from jax.experimental.pallas import tpu as pltpu
from jax.sharding import PartitionSpec as P

MESH = pl.DeviceIdType.MESH
LANES = 128
LEAD = 8


def round_up(value, step):
    return -(-value // step) * step


def gelu_tanh(values):
    return jax.nn.gelu(values, approximate=True)


def body(
    lats, n, rows, cols, chans, pad, reach,
    x_hbm, metric_ref, k1_ref, k2_ref, widths_ref, gains_ref, gain_ref, win_hbm, wout_hbm,
    out_ref,
    ext, sec, held, acc, mix, circ, zsend, zrecv, flatx, edge, edge_in, strip, strip_in, rim, rim_in,
    taps, lines, taps_one, win_ref, wout_ref, x_ref,
    w_sem,
    hs_sem, hr_sem, fs_sem, fr_sem, rs_sem, rr_sem,
):
    lat = lax.axis_index("lat")
    me = lax.axis_index("lon")
    chunks = rows // n
    half = n // 2
    wide = ext.shape[1]
    full = ext.shape[2]
    slabs = 2 * reach + 1

    at_top = lat == 0
    at_bottom = lat == lats - 1
    up_lat = jnp.where(at_top, 0, lat - 1)
    up_lon = jnp.where(at_top, lax.rem(me + half, n), me)
    down_lat = jnp.where(at_bottom, lats - 1, lat + 1)
    down_lon = jnp.where(at_bottom, lax.rem(me + half, n), me)
    left = lax.rem(me + n - 1, n)
    right = lax.rem(me + 1, n)

    def before(lon):
        return lax.rem(lon + n - 1, n)

    def after(lon):
        return lax.rem(lon + 1, n)

    loads = [
        pltpu.make_async_copy(x_hbm, x_ref, w_sem.at[2]),
        pltpu.make_async_copy(win_hbm, win_ref, w_sem.at[0]),
        pltpu.make_async_copy(wout_hbm, wout_ref, w_sem.at[1]),
    ]
    for load in loads:
        load.start()

    barrier = pltpu.get_barrier_semaphore()
    greeted = [
        (lat, left), (lat, right),
        (up_lat, up_lon), (up_lat, before(up_lon)), (up_lat, after(up_lon)),
        (down_lat, down_lon), (down_lat, before(down_lon)), (down_lat, after(down_lon)),
    ] + [(lat, lax.rem(me + o, n)) for o in range(1, n)]
    for device in greeted:
        pl.semaphore_signal(barrier, inc=1, device_id=device, device_id_type=MESH)
    def clear(e, carry):
        ext[e, 0:LEAD, :] = jnp.zeros((LEAD, full), jnp.float32)
        return carry

    lax.fori_loop(0, rows + 4, clear, 0)

    diagonal = lax.broadcasted_iota(jnp.int32, (pad, cols), 0) == lax.broadcasted_iota(
        jnp.int32, (pad, cols), 1
    )

    loads[0].wait()
    for c in range(chans // LANES):
        lanes = slice(c * LANES, (c + 1) * LANES)
        flatx[c] = x_ref[:, :, lanes].astype(jnp.float32).reshape(cols * rows, LANES)

    def place(i, carry):
        line = jnp.broadcast_to(metric_ref[pl.ds(i, 1), :], (pad, cols))
        column = jnp.sum(jnp.where(diagonal, line, 0.0), axis=1, keepdims=True)
        weight = jnp.broadcast_to(column, (pad, LANES))
        ext[i + 2, pad:wide, :] = jnp.zeros((wide - pad, full), jnp.float32)
        held[i, pad - 8:pad, :] = jnp.zeros((8, chans), jnp.float32)
        ext[i + 2, LEAD:wide, chans:] = weight
        rim[0, i] = weight[0:1]
        rim[1, i] = weight[cols - 1:cols]
        for c in range(chans // LANES):
            lanes = slice(c * LANES, (c + 1) * LANES)
            cells = flatx[c, pl.ds(i, cols, stride=rows), :]
            held[i, 0:cols, lanes] = cells
            first = (cells * weight[0:cols]).astype(jnp.bfloat16).astype(jnp.float32)
            ext[i + 2, LEAD:LEAD + cols, lanes] = first
            strip[0, i, :, lanes] = first[0:2].astype(jnp.bfloat16)
            strip[1, i, :, lanes] = first[cols - 2:cols].astype(jnp.bfloat16)
        return carry

    lax.fori_loop(0, rows, place, 0)
    for slot, row in enumerate((2, 3, rows, rows + 1)):
        edge[slot] = ext[row, LEAD:wide, 0:chans].astype(jnp.bfloat16)
    pl.semaphore_wait(barrier, len(greeted))

    halo = []

    def send_halo(src, dst, recv_index, device):
        copy = pltpu.make_async_remote_copy(
            src_ref=src, dst_ref=dst, send_sem=hs_sem.at[len(halo)], recv_sem=hr_sem.at[recv_index],
            device_id=device, device_id_type=MESH,
        )
        copy.start()
        halo.append(copy)

    def slot_row(slot):
        return jnp.where(slot < 2, slot, rows + slot)

    for s, device in ((0, left), (1, right)):
        send_halo(strip.at[s], strip_in.at[1 - s, pl.ds(2, rows)], 4 + s, (lat, device))
        send_halo(rim.at[s], rim_in.at[1 - s, pl.ds(2, rows)], 6 + s, (lat, device))
    for i in range(2):
        up_slot = jnp.where(at_top, 1 - i, 2 + i)
        down_slot = jnp.where(at_bottom, 3 - i, i)
        for slot, src_row, device_lat, device_lon in (
            (up_slot, i, up_lat, up_lon),
            (down_slot, rows - 2 + i, down_lat, down_lon),
        ):
            source = i if src_row < 2 else 2 + i
            dst_row = slot_row(slot)
            target = (device_lat, device_lon)
            send_halo(edge.at[source], edge_in.at[slot], slot, target)
            corners = ((0, before(device_lon)), (1, after(device_lon)))
            for s, corner_lon in corners:
                send_halo(
                    strip.at[s, src_row], strip_in.at[1 - s, dst_row], 8 + 4 * s + slot,
                    (device_lat, corner_lon),
                )
            if src_row in (0, rows - 1):
                near = jnp.where(slot < 2, 0, 1)
                send_halo(
                    ext.at[src_row + 2, pl.ds(LEAD, pad), pl.ds(chans, LANES)],
                    ext.at[dst_row, pl.ds(LEAD, pad), pl.ds(chans, LANES)],
                    16 + near, target,
                )
                for s, corner_lon in corners:
                    send_halo(
                        rim.at[s, src_row], rim_in.at[1 - s, dst_row], 18 + 2 * s + near,
                        (device_lat, corner_lon),
                    )

    tap_lanes = taps.shape[2]
    lane_ids = lax.broadcasted_iota(jnp.int32, (pad, tap_lanes), 1)
    taps_one[0, 0:9] = k1_ref[...]
    for a in range(3):
        taps_one[1, 3 * a:3 * a + 3] = k1_ref[6 - 3 * a:9 - 3 * a, :]
    count = gains_ref.shape[1]
    center = (count - 1) // 2
    lines[...] = jnp.zeros(lines.shape, jnp.float32)
    lines[:, 0:count] = gains_ref[...].astype(jnp.float32)
    for k in range(chunks):
        line = jnp.broadcast_to(lines[pl.ds(k * n + me, 1), :], (pad, tap_lanes))
        kept = jnp.abs(lane_ids - center) <= widths_ref[k * n + me]
        line = jnp.where(kept, line, 0.0)
        shifted = pltpu.roll(line, 0, 1, stride=1, stride_axis=0)
        total = jnp.zeros((pad, tap_lanes), jnp.float32)
        for d in range(slabs):
            moved = pltpu.roll(shifted, (pad - cols) * d, 1) if d else shifted
            inside = (lane_ids >= pad * d) & (lane_ids < pad * d + cols)
            total = jnp.where(inside, moved, total)
        taps[k] = total.astype(jnp.bfloat16)

    def recv_halo(src, dst, recv_index):
        pltpu.make_async_remote_copy(
            src_ref=src, dst_ref=dst, send_sem=hs_sem.at[0], recv_sem=hr_sem.at[recv_index],
            device_id=(lat, right), device_id_type=MESH,
        ).wait_recv()

    for s in range(2):
        recv_halo(strip.at[s], strip_in.at[1 - s, pl.ds(2, rows)], 4 + s)
        recv_halo(rim.at[s], rim_in.at[1 - s, pl.ds(2, rows)], 6 + s)
        row = (1, rows + 2)[s]
        recv_halo(
            ext.at[2, pl.ds(LEAD, pad), pl.ds(chans, LANES)],
            ext.at[row, pl.ds(LEAD, pad), pl.ds(chans, LANES)], 16 + s,
        )
        for near in range(2):
            recv_halo(rim.at[s, 0], rim_in.at[1 - s, (1, rows + 2)[near]], 18 + 2 * s + near)
    for slot in range(4):
        row = slot if slot < 2 else rows + slot
        recv_halo(edge.at[0], edge_in.at[slot], slot)
        for s in range(2):
            recv_halo(strip.at[s, 0], strip_in.at[1 - s, row], 8 + 4 * s + slot)
    for copy in halo:
        copy.wait_send()

    for slot in range(4):
        row = slot if slot < 2 else rows + slot
        ext[row, LEAD:wide, 0:chans] = edge_in[slot].astype(jnp.float32)

    def join(e, carry):
        for s, at in ((0, LEAD - 2), (1, LEAD + cols)):
            ext[e, at:at + 2, 0:chans] = strip_in[s, e].astype(jnp.float32)
        return carry

    def join_rim(e, carry):
        ext[e, LEAD - 1:LEAD, chans:] = rim_in[0, e]
        ext[e, LEAD + cols:LEAD + cols + 1, chans:] = rim_in[1, e]
        return carry

    lax.fori_loop(1, rows + 3, join_rim, 0)
    lax.fori_loop(0, rows + 4, join, 0)

    def stencil(src, row, kernel, lanes):
        sums = [None, None, None]
        for a in range(3):
            line = src[row + a, :, lanes]
            for b in range(3):
                term = kernel(a, b, lanes) * line
                sums[b] = term if sums[b] is None else sums[b] + term
        return pltpu.roll(sums[0], 1, 0) + sums[1] + pltpu.roll(sums[2], wide - 1, 0)

    def second_row(p, carry):
        flip = ((p == 0) & at_top) | ((p == rows + 1) & at_bottom)
        which = jnp.where(flip, 1, 0)
        weight = ext[p + 1, :, chans:]
        for c in range(chans // LANES):
            lanes = slice(c * LANES, (c + 1) * LANES)
            value = stencil(ext, p, lambda a, b, l: taps_one[which, 3 * a + b:3 * a + b + 1, l], lanes)
            value = weight * gelu_tanh(value)
            sec[p, :, lanes] = value.astype(jnp.bfloat16).astype(jnp.float32)
        return carry

    col_ids = lax.broadcasted_iota(jnp.int32, (pad, LANES), 0)

    def mixed_row(i, carry):
        for c in range(chans // LANES):
            lanes = slice(c * LANES, (c + 1) * LANES)
            value = stencil(sec, i, lambda a, b, l: k2_ref[3 * a + b:3 * a + b + 1, l], lanes)
            value = held[i, :, lanes] + value[LEAD:, :]
            mix[i, :, lanes] = jnp.where(col_ids < cols, value, 0.0).astype(jnp.bfloat16)
        return carry

    forward = []
    for k in range(chunks):
        start = 0 if k == 0 else k * n + 2
        lax.fori_loop(start, (k + 1) * n + 2, second_row, 0)
        lax.fori_loop(k * n, (k + 1) * n, mixed_row, 0)
        for o in range(1, n):
            target = lax.rem(me + o, n)
            copy = pltpu.make_async_remote_copy(
                src_ref=mix.at[k * n + target], dst_ref=circ.at[k, me + reach],
                send_sem=fs_sem.at[k, o], recv_sem=fr_sem.at[k, o],
                device_id=(lat, target), device_id_type=MESH,
            )
            copy.start()
            forward.append(copy)
        circ[k, me + reach] = mix[k * n + me]

    for load in loads[1:]:
        load.wait()

    group = 8

    def network(g, carry):
        flat = mix[pl.ds(g * group, group)].reshape(group * pad, chans).astype(jnp.float32)
        scale = lax.rsqrt(jnp.mean(flat * flat, axis=1, keepdims=True) + 1e-06)
        normed = (flat * scale * gain_ref[...]).astype(jnp.bfloat16)
        hidden = gelu_tanh(
            jnp.dot(normed, win_ref[...], preferred_element_type=jnp.float32)
        ).astype(jnp.bfloat16)
        point = jnp.dot(hidden, wout_ref[...], preferred_element_type=jnp.float32)
        acc[pl.ds(g * group, group)] = (flat + point).reshape(group, pad, chans)
        return carry

    lax.fori_loop(0, rows // group, network, 0)

    back = []
    for k in range(chunks):
        for o in range(1, n):
            source = lax.rem(me + n - o, n)
            pltpu.make_async_remote_copy(
                src_ref=mix.at[k * n], dst_ref=circ.at[k, source + reach],
                send_sem=fs_sem.at[k, o], recv_sem=fr_sem.at[k, o],
                device_id=(lat, source), device_id_type=MESH,
            ).wait_recv()
        for e in range(reach):
            circ[k, e] = circ[k, n + e]
            circ[k, n + reach + e] = circ[k, reach + e]

        def filter_block(a, carry):
            window = circ[k, pl.ds(a, slabs)].reshape(slabs * pad, chans)
            result = jnp.dot(
                taps[k, :, 0:slabs * pad], window, preferred_element_type=jnp.float32
            )
            zsend[k * n + a] = result.astype(jnp.bfloat16)
            return carry

        lax.fori_loop(0, n, filter_block, 0, unroll=4)
        for o in range(1, n):
            target = lax.rem(me + o, n)
            copy = pltpu.make_async_remote_copy(
                src_ref=zsend.at[k * n + target], dst_ref=zrecv.at[k * n + me],
                send_sem=rs_sem.at[k, o], recv_sem=rr_sem.at[k, o],
                device_id=(lat, target), device_id_type=MESH,
            )
            copy.start()
            back.append(copy)
        zrecv[k * n + me] = zsend[k * n + me]

    for k in range(chunks):
        for o in range(1, n):
            source = lax.rem(me + n - o, n)
            pltpu.make_async_remote_copy(
                src_ref=zsend.at[k * n], dst_ref=zrecv.at[k * n + source],
                send_sem=rs_sem.at[k, o], recv_sem=rr_sem.at[k, o],
                device_id=(lat, source), device_id_type=MESH,
            ).wait_recv()

        def finish(i, carry):
            out_ref[i] = (acc[i] + zrecv[i].astype(jnp.float32)).astype(jnp.bfloat16)
            return carry

        lax.fori_loop(k * n, (k + 1) * n, finish, 0)

    for copy in forward + back:
        copy.wait_send()


def local(
    lats, n,
    inputs, metric, kernel_one, kernel_two, widths, zonal_gains, norm_gain, weight_in, weight_out
):
    rows, cols, chans = inputs.shape
    pad = round_up(cols, 16)
    wide = LEAD + pad
    full = chans + LANES
    reach = n // 4
    slabs = 2 * reach + 1
    count = zonal_gains.shape[1]
    tap_lanes = round_up(max(slabs * pad, count + pad - 1), LANES)

    chunks = rows // n
    vmem = pl.BlockSpec(memory_space=pltpu.VMEM)
    sem = pltpu.SemaphoreType.DMA
    out = pl.pallas_call(
        functools.partial(body, lats, n, rows, cols, chans, pad, reach),
        out_shape=jax.ShapeDtypeStruct((rows, pad, chans), jnp.bfloat16),
        in_specs=[pl.BlockSpec(memory_space=pl.ANY)] + [vmem] * 3
        + [pl.BlockSpec(memory_space=pltpu.SMEM), vmem, vmem]
        + [pl.BlockSpec(memory_space=pl.ANY)] * 2,
        out_specs=vmem,
        scratch_shapes=[
            pltpu.VMEM((rows + 4, wide, full), jnp.float32),
            pltpu.VMEM((rows + 2, wide, chans), jnp.float32),
            pltpu.VMEM((rows, pad, chans), jnp.float32),
            pltpu.VMEM((rows, pad, chans), jnp.float32),
            pltpu.VMEM((rows, pad, chans), jnp.bfloat16),
            pltpu.VMEM((chunks, n + 2 * reach, pad, chans), jnp.bfloat16),
            pltpu.VMEM((rows, pad, chans), jnp.bfloat16),
            pltpu.VMEM((rows, pad, chans), jnp.bfloat16),
            pltpu.VMEM((chans // LANES, cols * rows, LANES), jnp.float32),
            pltpu.VMEM((4, pad, chans), jnp.bfloat16),
            pltpu.VMEM((4, pad, chans), jnp.bfloat16),
            pltpu.VMEM((2, rows, 2, chans), jnp.bfloat16),
            pltpu.VMEM((2, rows + 4, 2, chans), jnp.bfloat16),
            pltpu.VMEM((2, rows, 1, LANES), jnp.float32),
            pltpu.VMEM((2, rows + 4, 1, LANES), jnp.float32),
            pltpu.VMEM((chunks, pad, tap_lanes), jnp.bfloat16),
            pltpu.VMEM((rows, tap_lanes), jnp.float32),
            pltpu.VMEM((2, 16, chans), jnp.float32),
            pltpu.VMEM(weight_in.shape, jnp.bfloat16),
            pltpu.VMEM(weight_out.shape, jnp.bfloat16),
            pltpu.VMEM((cols, rows, chans), jnp.bfloat16),
            sem((3,)),
            sem((22,)), sem((22,)),
            sem((chunks, n)), sem((chunks, n)), sem((chunks, n)), sem((chunks, n)),
        ],
        compiler_params=pltpu.CompilerParams(
            collective_id=0, has_side_effects=True, vmem_limit_bytes=60 * 2**20
        ),
    )(
        inputs.transpose(1, 0, 2), metric, kernel_one, kernel_two, widths, zonal_gains, norm_gain.reshape(1, chans),
        weight_in, weight_out,
    )
    return out[:, :cols]


def solution(mesh):
    placed = (
        P("lat", "lon", None),
        P("lat", "lon"),
        P(),
        P(),
        P("lat"),
        P("lat", None),
        P(),
        P(),
        P(),
    )
    return jax.shard_map(
        functools.partial(local, mesh.shape["lat"], mesh.shape["lon"]),
        mesh=mesh, in_specs=placed, out_specs=P("lat", "lon", None), check_vma=False,
    )
```
